512 devices in a mesh: ctx: 64 (over x, z), ch: 8 (over y, core).
Axes of the slice: x: 4, y: 4, z: 16, core: 2. Of those that a mesh axis runs over, the one named last changes fastest.
Arguments:
- q_proj: bfloat16 [16384, 4096], P('ctx', 'ch'), may hold values from -6 to 6
- k_proj: bfloat16 [16384, 4096], P('ctx', 'ch'), may hold values from -6 to 6
- v_proj: bfloat16 [16384, 4096], P('ctx', 'ch'), may hold values from -6 to 6
- residue: float32 [16, 4096], P(None, 'ch'), may hold values from -4 to 4
- rate: float32 [16, 4096], P(None, 'ch'), may hold values from 1.2207031e-05 to 0.1
- skip: float32 [4096], P('ch'), may hold values from -4 to 4
- w_out: bfloat16 [4096, 6144], P('ctx', 'ch'), may hold values from -0.09375 to 0.09375
Outputs:
- mixed: bfloat16 [16384, 6144], P('ctx', 'ch')
The draws below stay inside these ranges and needn't reach their ends.
All inputs are finite; a program needn't handle non-finite values.
Results may differ from the reference program's by a relative error of at most 0.0049.
Values may be sent and summed in bfloat16 or wider, within the bound.
A program may use at most 128 MiB of HBM per device.

```python
import math
import jax
import jax.numpy as jnp
from jax import lax

D = 6144
SLAB = 4096
MODES = 16
SEQ = 16384


def draw_rate(key, part):
    key_pick, key_fast, key_middle, key_slow = jax.random.split(jax.random.fold_in(key, 7), 4)
    shape = (MODES, SLAB)
    picks = jax.random.randint(key_pick, shape, 0, 8)
    fast_pick = picks < 3
    middle_pick = jnp.logical_and(picks >= 3, picks < 6)
    fast_rate = jnp.exp(jax.random.uniform(key_fast, shape, jnp.float32, jnp.log(0.02), jnp.log(0.1)))
    middle_rate = jnp.exp(jax.random.uniform(key_middle, shape, jnp.float32, jnp.log(2.0 / SEQ), jnp.log(0.02)))
    slow_rate = jnp.exp(jax.random.uniform(key_slow, shape, jnp.float32, jnp.log(0.2 / SEQ), jnp.log(2.0 / SEQ)))
    chosen = jnp.where(fast_pick, fast_rate, jnp.where(middle_pick, middle_rate, slow_rate))
    return chosen.astype(jnp.float32)


def shard_levels(own_key, dims, shards, least, high):
    loudness = 1.0
    for dim, shards_of in shards:
        steps = jax.random.uniform(jax.random.fold_in(jax.random.fold_in(own_key, 6), dim), (shards_of,), jnp.float32, least / len(shards), high / len(shards))
        loudness = loudness * jnp.repeat(jnp.exp(steps), dims[dim] // shards_of).reshape((-1,) + (1,) * (len(dims) - 1 - dim))
    return loudness


def bell_draw(stream_key, shape, scale, most, pieces=(), kind=jnp.bfloat16):
    factor_of = shard_levels(stream_key, shape, pieces, -0.22, 0.18) if pieces else 1.0
    values = jax.random.normal(stream_key, shape, jnp.float32) * scale * factor_of
    return jnp.minimum(jnp.maximum(values, -most), most).astype(kind)


def setup_inputs(seed: int = 0) -> dict:
    keys = jax.random.split(jax.random.key(seed), 8)
    return {
        "q_proj": bell_draw(keys[0], (SEQ, SLAB), 1.0, 6.0, ((0, 64), (1, 8))),
        "k_proj": bell_draw(keys[1], (SEQ, SLAB), 1.0, 6.0, ((0, 64), (1, 8))),
        "v_proj": bell_draw(keys[2], (SEQ, SLAB), 1.0, 6.0, ((0, 64), (1, 8))),
        "residue": bell_draw(keys[3], (MODES, SLAB), 1.0, 4.0, ((1, 8),), jnp.float32),
        "rate": draw_rate(jax.random.fold_in(keys[7], 71), 0),
        "skip": bell_draw(keys[5], (SLAB,), 1.0, 4.0, ((0, 8),), jnp.float32),
        "w_out": bell_draw(keys[6], (SLAB, D), SLAB ** -0.5, 0.09375, ((0, 64), (1, 8))),
    }


def filter_block(operands):
    signal_block, coefficient_block, rate_block = operands
    position = jnp.arange(SEQ).astype(jnp.float32)
    filt = jnp.zeros(signal_block.shape, jnp.float32)
    for mode_index in range(MODES):
        filt = filt + coefficient_block[mode_index][None, :] * jnp.exp(-rate_block[mode_index][None, :] * position[:, None])
    length = 2 * SEQ
    spectrum = jnp.fft.rfft(signal_block, n=length, axis=0) * jnp.fft.rfft(filt, n=length, axis=0)
    return jnp.fft.irfft(spectrum, n=length, axis=0)[:SEQ]

def reference(q_proj, k_proj, v_proj, residue, rate, skip, w_out):
    signal = k_proj.astype(jnp.float32) * v_proj.astype(jnp.float32)
    coefficient = residue * jnp.sqrt(2.0 * rate)
    width = math.gcd(SLAB, 128)
    blocks = SLAB // width
    signal_blocks = signal.reshape(SEQ, blocks, width).transpose(1, 0, 2)
    coefficient_blocks = coefficient.reshape(MODES, blocks, width).transpose(1, 0, 2)
    rate_blocks = rate.reshape(MODES, blocks, width).transpose(1, 0, 2)
    conv = lax.map(filter_block, (signal_blocks, coefficient_blocks, rate_blocks))
    conv = conv.transpose(1, 0, 2).reshape(SEQ, SLAB)
    conv = conv + skip[None, :] * signal
    gated = (q_proj.astype(jnp.float32) * conv).astype(jnp.bfloat16)
    row_block = math.gcd(SEQ, 4096)

    def project(rows_in):
        return jnp.dot(rows_in, w_out, preferred_element_type=jnp.float32).astype(jnp.bfloat16)
    mixed = lax.map(project, gated.reshape(SEQ // row_block, row_block, SLAB))
    return mixed.reshape(SEQ, D)
```

```python
import jax
import jax.numpy as jnp
from jax import lax
from jax.experimental import pallas as pl
from jax.experimental.pallas import tpu as pltpu
from jax.sharding import PartitionSpec as P

MESH = pl.DeviceIdType.MESH
NX, NZ, NY, NC = 4, 16, 4, 2
ROWS, CH, MODES = 256, 512, 16
WROWS, COLS, PCOLS = 64, 768, 256
GROUPS, CHUNKS, LEN = 4, 8, 32
PR, PL, QR, QL = 8, 7, 7, 8
PS, QS = pl.ds(0, PCOLS), pl.ds(PCOLS, COLS - PCOLS)
F32, BF16 = jnp.float32, jnp.bfloat16


def kernel(
    q_hbm, k_hbm, v_hbm, w_hbm, residue, rate, skip, out,
    q, k, v, w, a, sig, y_buf, carry, acc, decay, coef,
    ends, got_ends, totals, states, got_states, pref,
    load_sem, st_send, st_recv, w_send, w_recv, a_send, a_recv,
):
    ctx, ch = lax.axis_index("ctx"), lax.axis_index("ch")
    x, z = ctx // NZ, ctx % NZ
    y, core = ch // NC, ch % NC
    xp, xm, x2 = (x + 1) % NX, (x + 3) % NX, (x + 2) % NX
    zp, zm = (z + 1) % NZ, (z + NZ - 1) % NZ
    yp, ym, y2 = (y + 1) % NY, (y + 3) % NY, (y + 2) % NY

    def at(x_to=None, z_to=None, ch_to=None):
        x_to = x if x_to is None else x_to
        z_to = z if z_to is None else z_to
        return (x_to * NZ + z_to, ch if ch_to is None else ch_to)

    def remote(src, dst, send, recv, where):
        return pltpu.make_async_remote_copy(
            src_ref=src, dst_ref=dst, send_sem=send, recv_sem=recv,
            device_id=where, device_id_type=MESH,
        )

    loads = [
        pltpu.make_async_copy(k_hbm, k, load_sem.at[0]),
        pltpu.make_async_copy(v_hbm, v, load_sem.at[1]),
        pltpu.make_async_copy(w_hbm, w.at[z, x], load_sem.at[2]),
        pltpu.make_async_copy(q_hbm, q, load_sem.at[3]),
    ]
    for c in loads:
        c.start()

    barrier = pltpu.get_barrier_semaphore()
    greet = [at(z_to=(z + i) % NZ) for i in range(1, NZ)]
    greet += [at(x_to=t) for t in (xp, xm, x2)]
    greet += [at(ch_to=yp * NC + core), at(ch_to=ym * NC + core), at(ch_to=y * NC + 1 - core)]
    for d in greet:
        pl.semaphore_signal(barrier, inc=1, device_id=d, device_id_type=MESH)

    decay[...] = jnp.exp(-rate[...])
    coef[...] = residue[...] * jnp.sqrt(2.0 * rate[...])
    loads[0].wait()
    loads[1].wait()
    chunk = lax.broadcasted_iota(jnp.int32, (CHUNKS, 128), 0)
    chunk_f = chunk.astype(F32)

    def rows_of(ref, m, lanes):
        return jnp.broadcast_to(ref[m : m + 1, lanes], (CHUNKS, 128))

    def shifted(val, n):
        return jnp.where(chunk >= n, pltpu.roll(val, n, 0), 0.0)

    for g in range(GROUPS):
        lanes = slice(g * 128, (g + 1) * 128)
        sig[g] = k[:, lanes].astype(F32) * v[:, lanes].astype(F32)
        ds = [rows_of(decay, m, lanes) for m in range(MODES)]

        def scan1(o, hs, g=g, ds=ds):
            for u in range(4):
                s = sig[g, pl.ds(o * 4 + u, CHUNKS, stride=LEN), :]
                hs = [d * h + s for d, h in zip(ds, hs)]
            return hs

        hs = lax.fori_loop(0, LEN // 4, scan1, [jnp.zeros((CHUNKS, 128), F32)] * MODES)
        for m in range(MODES):
            r = rows_of(rate, m, lanes) * float(LEN)
            end = jnp.sum(hs[m] * jnp.exp(-r * (CHUNKS - 1.0 - chunk_f)), axis=0, keepdims=True)
            ends[m, 0:1, lanes] = end
            c1 = jnp.exp(-r)
            val = shifted(hs[m], 1)
            val = val + c1 * shifted(val, 1)
            c2 = c1 * c1
            val = val + c2 * shifted(val, 2)
            val = val + (c2 * c2) * shifted(val, 4)
            carry[g, m] = val

    got_ends[z] = ends[z]
    loads[2].wait()
    pl.semaphore_wait(barrier, len(greet))

    def all_z(src, dst, n):
        def one(i, _):
            to = (z + i) % NZ
            remote(src.at[to], dst.at[z], st_send.at[n], st_recv.at[n], at(z_to=to)).start()
            return 0

        lax.fori_loop(1, NZ, one, 0)

    def settle(ref, count, sem):
        part = ref.at[pl.ds(0, count)]
        pltpu.make_async_copy(part, part, sem).wait()

    all_z(ends, got_ends, 0)

    keys = {}

    def slot(key):
        return keys.setdefault(key, len(keys))

    pending = []

    def w_copy(key, part, where):
        n = slot(key)
        return remote(part, part, w_send.at[n], w_recv.at[n], where)

    def send(key, part, where):
        c = w_copy(key, part, where)
        c.start()
        pending.append(c)

    def arrived(key, part):
        w_copy(key, part, at(z_to=zp)).wait_recv()

    def q_part(z_at, x_at):
        return w.at[z_at, x_at, :, QS]

    def p_part(z_at):
        return w.at[z_at, :, :, PS]

    def back(s):
        return (z + NZ - s) % NZ

    def ahead(s):
        return (z + s) % NZ

    def across(way, s, z_at):
        part = q_part(z_at, x)
        send(("x+", way, s), part, at(x_to=xp))
        send(("x-", way, s), part, at(x_to=xm))

    def relay(way, s):
        if way == "r":
            z_at = back(s)
            part = q_part(z_at, xm)
            arrived(("x+", way, s), part)
            send(("x2", way, s), part, at(x_to=xp))
        else:
            z_at = ahead(s)
            part = q_part(z_at, xp)
            arrived(("x-", way, s), part)
            send(("x2", way, s), part, at(x_to=xm))

    def q_step(s):
        if s <= QR:
            if s:
                arrived(("qr", s - 1), q_part(back(s), x))
            if s < QR:
                send(("qr", s), q_part(back(s), x), at(z_to=zp))
        if s <= QL:
            if s:
                arrived(("ql", s - 1), q_part(ahead(s), x))
            if s < QL:
                send(("ql", s), q_part(ahead(s), x), at(z_to=zm))
        if s <= QR:
            across("r", s, back(s))
        if 0 < s <= QL:
            across("l", s, ahead(s))

    def p_step(s):
        if s <= PR:
            if s:
                arrived(("pr", s - 1), p_part(back(s)))
            if s < PR:
                send(("pr", s), p_part(back(s)), at(z_to=zp))
        if s <= PL:
            if s:
                arrived(("pl", s - 1), p_part(ahead(s)))
            if s < PL:
                send(("pl", s), p_part(ahead(s)), at(z_to=zm))

    def relay_step(s):
        if s <= QR:
            relay("r", s)
        if 0 < s <= QL:
            relay("l", s)

    def w_step(s):
        q_step(s)
        p_step(s)
        relay_step(s - 1)

    q_step(0)
    for key, x_to in (("p+", xp), ("p-", xm), ("p2", x2)):
        send((key,), w.at[z, x, :, PS], at(x_to=x_to))
    for key, x_from in (("p+", xm), ("p-", xp), ("p2", x2)):
        arrived((key,), w.at[z, x_from, :, PS])
    p_step(0)
    w_step(1)

    settle(got_ends, NZ - 1, st_recv.at[0])
    own_rate = rate[pl.ds(z, 1), :]
    step_decay = jnp.exp(-own_rate * float(ROWS))
    total = jnp.zeros((1, CH), F32)
    for i in range(NZ):
        pref[i] = total
        total = step_decay * total + got_ends[i]
    totals[x] = total
    for t in (xp, xm, x2):
        remote(totals.at[x], totals.at[x], st_send.at[1], st_recv.at[1], at(x_to=t)).start()
    w_step(2)
    settle(totals, NX - 1, st_recv.at[1])
    entering = jnp.zeros((1, CH), F32)
    for i in range(NX):
        gap = jnp.maximum(x - 1 - i, 0).astype(F32)
        used = jnp.where(i < x, 1.0, 0.0)
        entering = entering + used * jnp.exp(-own_rate * (float(ROWS * NZ) * gap)) * totals[i]
    for i in range(NZ):
        states[i] = pref[i] + jnp.exp(-own_rate * float(ROWS * i)) * entering
    got_states[z] = states[z]
    all_z(states, got_states, 2)
    w_step(3)
    w_step(4)
    settle(got_states, NZ - 1, st_recv.at[2])
    loads[3].wait()

    a_pending = []
    partner = at(ch_to=y * NC + 1 - core)

    def a_copy(kind, g, block, where):
        part = a.at[block, g]
        return remote(part, part, a_send.at[kind, g], a_recv.at[kind, g], where)

    def a_go(kind, g, block, where):
        c = a_copy(kind, g, block, where)
        c.start()
        a_pending.append(c)

    up, down, far = at(ch_to=yp * NC + core), at(ch_to=ym * NC + core), y2 * NC + core
    from_up, from_down = yp * NC + core, ym * NC + core

    def a_make(g):
        lanes = slice(g * 128, (g + 1) * 128)
        ds = [rows_of(decay, m, lanes) for m in range(MODES)]
        cs = [rows_of(coef, m, lanes) for m in range(MODES)]
        hs = []
        for m in range(MODES):
            r = rows_of(rate, m, lanes) * float(LEN)
            into = jnp.broadcast_to(got_states[m, 0:1, lanes], (CHUNKS, 128))
            hs.append(carry[g, m] + jnp.exp(-r * chunk_f) * into)

        def scan2(o, hs):
            for u in range(2):
                where = pl.ds(o * 2 + u, CHUNKS, stride=LEN)
                s = sig[g, where, :]
                hs = [d * h + s for d, h in zip(ds, hs)]
                terms = [c * h for c, h in zip(cs, hs)]
                while len(terms) > 1:
                    terms = [p + r for p, r in zip(terms[::2], terms[1::2])]
                y_buf[where, :] = terms[0]
            return hs

        lax.fori_loop(0, LEN // 2, scan2, hs)
        conv = y_buf[...] + skip[0:1, lanes] * sig[g]
        a[ch, g] = (q[:, lanes].astype(F32) * conv).astype(BF16)
        a_go(1, g, ch, up)
        a_go(2, g, ch, down)
        a_go(0, g, ch, partner)

    def a_pass(g):
        a_copy(1, g, from_down, up).wait_recv()
        if g % 2 == 0:
            a_go(3, g, from_down, up)
        a_go(4, g, from_down, partner)
        a_copy(2, g, from_up, up).wait_recv()
        if g % 2 == 1:
            a_go(3, g, from_up, down)
        a_go(5, g, from_up, partner)

    def a_last(g):
        a_copy(3, g, far, up).wait_recv()
        a_go(6, g, far, partner)

    a_make(0)
    a_make(1)
    w_step(5)
    a_make(2)
    a_make(3)
    a_pass(0)
    w_step(6)
    a_pass(1)
    a_pass(2)
    a_last(0)
    w_step(7)
    a_pass(3)
    a_last(1)
    a_last(2)
    w_step(8)
    a_last(3)
    relay_step(8)

    for s in range(QR + 1):
        arrived(("x-", "r", s), q_part(back(s), xp))
        arrived(("x2", "r", s), q_part(back(s), x2))
    for s in range(1, QL + 1):
        arrived(("x+", "l", s), q_part(ahead(s), xm))
        arrived(("x2", "l", s), q_part(ahead(s), x2))
    other = 1 - core
    for kind, block in ((0, y), (4, ym), (5, yp), (6, y2)):
        for g in range(GROUPS):
            a_copy(kind, g, block * NC + other, partner).wait_recv()

    def multiply(j, _):
        left = jnp.concatenate([a[j, g] for g in range(GROUPS)], axis=1)
        first, x_at = (j % 2) * 8, j // 2
        for n in range(COLS // 256):
            cols = slice(n * 256, (n + 1) * 256)
            right = w[pl.ds(first, 8), x_at, :, cols].reshape(8 * WROWS, 256)
            acc[:, cols] += jnp.dot(left, right, preferred_element_type=F32)
        return 0

    acc[...] = jnp.zeros_like(acc)
    lax.fori_loop(0, NY * NC, multiply, 0)
    out[...] = acc[...].astype(BF16)

    settle(got_ends, NZ - 1, st_send.at[0])
    settle(totals, NX - 1, st_send.at[1])
    settle(got_states, NZ - 1, st_send.at[2])
    for c in pending + a_pending:
        c.wait_send()


def body(q_proj, k_proj, v_proj, residue, rate, skip, w_out):
    vmem = pl.BlockSpec(memory_space=pltpu.VMEM)
    hbm = pl.BlockSpec(memory_space=pl.ANY)
    dma = pltpu.SemaphoreType.DMA
    n_w = PR + PL + QR + QL + 3 * NZ + 3
    row = (1, CH)
    return pl.pallas_call(
        kernel,
        out_shape=jax.ShapeDtypeStruct((ROWS, COLS), BF16),
        in_specs=[hbm] * 4 + [vmem] * 3,
        out_specs=vmem,
        scratch_shapes=[
            pltpu.VMEM((ROWS, CH), BF16),
            pltpu.VMEM((ROWS, CH), BF16),
            pltpu.VMEM((ROWS, CH), BF16),
            pltpu.VMEM((NZ, NX, WROWS, COLS), BF16),
            pltpu.VMEM((NY * NC, GROUPS, ROWS, 128), BF16),
            pltpu.VMEM((GROUPS, ROWS, 128), F32),
            pltpu.VMEM((ROWS, 128), F32),
            pltpu.VMEM((GROUPS, MODES, CHUNKS, 128), F32),
            pltpu.VMEM((ROWS, COLS), F32),
            pltpu.VMEM((MODES, CH), F32),
            pltpu.VMEM((MODES, CH), F32),
            pltpu.VMEM((MODES,) + row, F32),
            pltpu.VMEM((NZ,) + row, F32),
            pltpu.VMEM((NX,) + row, F32),
            pltpu.VMEM((NZ,) + row, F32),
            pltpu.VMEM((MODES,) + row, F32),
            pltpu.VMEM((NZ,) + row, F32),
            dma((4,)),
            dma((3,)),
            dma((3,)),
            dma((n_w,)),
            dma((n_w,)),
            dma((7, GROUPS)),
            dma((7, GROUPS)),
        ],
        compiler_params=pltpu.CompilerParams(
            collective_id=0, has_side_effects=True, vmem_limit_bytes=48 * 2**20
        ),
    )(q_proj, k_proj, v_proj, w_out, residue, rate, skip.reshape(1, CH))


def solution(mesh):
    placed = (
        P("ctx", "ch"),
        P("ctx", "ch"),
        P("ctx", "ch"),
        P(None, "ch"),
        P(None, "ch"),
        P("ch"),
        P("ctx", "ch"),
    )
    return jax.shard_map(
        body, mesh=mesh, in_specs=placed, out_specs=P("ctx", "ch"), check_vma=False
    )
```

```python
import jax
import jax.numpy as jnp
from jax import lax
from jax.experimental import pallas as pl
from jax.experimental.pallas import tpu as pltpu
from jax.sharding import PartitionSpec as P

MESH = pl.DeviceIdType.MESH
NX, NZ, NY, NC = 4, 16, 4, 2
ROWS, CH, MODES = 256, 512, 16
WROWS, COLS, PCOLS = 64, 768, 256
GROUPS, CHUNKS, LEN = 4, 8, 32
PR, PL, QR, QL = 8, 7, 7, 8
PS, QS = pl.ds(0, PCOLS), pl.ds(PCOLS, COLS - PCOLS)
F32, BF16 = jnp.float32, jnp.bfloat16


def kernel(
    q_hbm, k_hbm, v_hbm, w_hbm, residue_hbm, rate_hbm, skip_hbm, out,
    q, k, v, residue, rate, skip, w, a, sig, y_buf, carry, acc, decay, coef,
    ends, got_ends, totals, states, got_states, pref,
    load_sem, st_send, st_recv, w_send, w_recv, a_send, a_recv,
):
    ctx, ch = lax.axis_index("ctx"), lax.axis_index("ch")
    x, z = ctx // NZ, ctx % NZ
    y, core = ch // NC, ch % NC
    xp, xm, x2 = (x + 1) % NX, (x + 3) % NX, (x + 2) % NX
    zp, zm = (z + 1) % NZ, (z + NZ - 1) % NZ
    yp, ym, y2 = (y + 1) % NY, (y + 3) % NY, (y + 2) % NY

    def at(x_to=None, z_to=None, ch_to=None):
        x_to = x if x_to is None else x_to
        z_to = z if z_to is None else z_to
        return (x_to * NZ + z_to, ch if ch_to is None else ch_to)

    def remote(src, dst, send, recv, where):
        return pltpu.make_async_remote_copy(
            src_ref=src, dst_ref=dst, send_sem=send, recv_sem=recv,
            device_id=where, device_id_type=MESH,
        )

    loads = [
        pltpu.make_async_copy(k_hbm, k, load_sem.at[0]),
        pltpu.make_async_copy(v_hbm, v, load_sem.at[1]),
        pltpu.make_async_copy(w_hbm, w.at[z, x], load_sem.at[2]),
        pltpu.make_async_copy(q_hbm, q, load_sem.at[3]),
        pltpu.make_async_copy(rate_hbm, rate, load_sem.at[4]),
        pltpu.make_async_copy(residue_hbm, residue, load_sem.at[5]),
        pltpu.make_async_copy(skip_hbm, skip, load_sem.at[6]),
    ]
    for c in loads:
        c.start()

    barrier = pltpu.get_barrier_semaphore()
    greet = [at(z_to=(z + i) % NZ) for i in range(1, NZ)]
    greet += [at(x_to=t) for t in (xp, xm, x2)]
    greet += [at(ch_to=yp * NC + core), at(ch_to=ym * NC + core), at(ch_to=y * NC + 1 - core)]
    for d in greet:
        pl.semaphore_signal(barrier, inc=1, device_id=d, device_id_type=MESH)

    loads[4].wait()
    decay[...] = jnp.exp(-rate[...])
    loads[0].wait()
    loads[1].wait()
    chunk = lax.broadcasted_iota(jnp.int32, (CHUNKS, 128), 0)
    chunk_f = chunk.astype(F32)

    def rows_of(ref, m, lanes):
        return jnp.broadcast_to(ref[m : m + 1, lanes], (CHUNKS, 128))

    def shifted(val, n):
        return jnp.where(chunk >= n, pltpu.roll(val, n, 0), 0.0)

    for g in range(GROUPS):
        lanes = slice(g * 128, (g + 1) * 128)
        sig[g] = k[:, lanes].astype(F32) * v[:, lanes].astype(F32)
        ds = [rows_of(decay, m, lanes) for m in range(MODES)]

        def scan1(o, hs, g=g, ds=ds):
            for u in range(4):
                s = sig[g, pl.ds(o * 4 + u, CHUNKS, stride=LEN), :]
                hs = [d * h + s for d, h in zip(ds, hs)]
            return hs

        hs = lax.fori_loop(0, LEN // 4, scan1, [jnp.zeros((CHUNKS, 128), F32)] * MODES)
        for m in range(MODES):
            r = rows_of(rate, m, lanes) * float(LEN)
            end = jnp.sum(hs[m] * jnp.exp(-r * (CHUNKS - 1.0 - chunk_f)), axis=0, keepdims=True)
            ends[m, 0:1, lanes] = end
            c1 = jnp.exp(-r)
            val = shifted(hs[m], 1)
            val = val + c1 * shifted(val, 1)
            c2 = c1 * c1
            val = val + c2 * shifted(val, 2)
            val = val + (c2 * c2) * shifted(val, 4)
            carry[g, m] = val

    got_ends[z] = ends[z]
    loads[2].wait()
    pl.semaphore_wait(barrier, len(greet))

    def all_z(src, dst, n):
        def one(i, _):
            to = (z + i) % NZ
            remote(src.at[to], dst.at[z], st_send.at[n], st_recv.at[n], at(z_to=to)).start()
            return 0

        lax.fori_loop(1, NZ, one, 0)

    def settle(ref, count, sem):
        part = ref.at[pl.ds(0, count)]
        pltpu.make_async_copy(part, part, sem).wait()

    all_z(ends, got_ends, 0)

    keys = {}

    def slot(key):
        return keys.setdefault(key, len(keys))

    pending = []

    def w_copy(key, part, where):
        n = slot(key)
        return remote(part, part, w_send.at[n], w_recv.at[n], where)

    def send(key, part, where):
        c = w_copy(key, part, where)
        c.start()
        pending.append(c)

    def arrived(key, part):
        w_copy(key, part, at(z_to=zp)).wait_recv()

    def q_part(z_at, x_at):
        return w.at[z_at, x_at, :, QS]

    def p_part(z_at):
        return w.at[z_at, :, :, PS]

    def back(s):
        return (z + NZ - s) % NZ

    def ahead(s):
        return (z + s) % NZ

    def across(way, s, z_at):
        part = q_part(z_at, x)
        send(("x+", way, s), part, at(x_to=xp))
        send(("x-", way, s), part, at(x_to=xm))

    def relay(way, s):
        if way == "r":
            z_at = back(s)
            part = q_part(z_at, xm)
            arrived(("x+", way, s), part)
            send(("x2", way, s), part, at(x_to=xp))
        else:
            z_at = ahead(s)
            part = q_part(z_at, xp)
            arrived(("x-", way, s), part)
            send(("x2", way, s), part, at(x_to=xm))

    def q_step(s):
        if s <= QR:
            if s:
                arrived(("qr", s - 1), q_part(back(s), x))
            if s < QR:
                send(("qr", s), q_part(back(s), x), at(z_to=zp))
        if s <= QL:
            if s:
                arrived(("ql", s - 1), q_part(ahead(s), x))
            if s < QL:
                send(("ql", s), q_part(ahead(s), x), at(z_to=zm))
        if s <= QR:
            across("r", s, back(s))
        if 0 < s <= QL:
            across("l", s, ahead(s))

    def p_step(s):
        if s <= PR:
            if s:
                arrived(("pr", s - 1), p_part(back(s)))
            if s < PR:
                send(("pr", s), p_part(back(s)), at(z_to=zp))
        if s <= PL:
            if s:
                arrived(("pl", s - 1), p_part(ahead(s)))
            if s < PL:
                send(("pl", s), p_part(ahead(s)), at(z_to=zm))

    def relay_step(s):
        if s <= QR:
            relay("r", s)
        if 0 < s <= QL:
            relay("l", s)

    def w_step(s):
        q_step(s)
        p_step(s)
        relay_step(s - 1)

    q_step(0)
    for key, x_to in (("p+", xp), ("p-", xm), ("p2", x2)):
        send((key,), w.at[z, x, :, PS], at(x_to=x_to))
    for key, x_from in (("p+", xm), ("p-", xp), ("p2", x2)):
        arrived((key,), w.at[z, x_from, :, PS])
    p_step(0)
    w_step(1)

    settle(got_ends, NZ - 1, st_recv.at[0])
    own_rate = rate[pl.ds(z, 1), :]
    step_decay = jnp.exp(-own_rate * float(ROWS))
    total = jnp.zeros((1, CH), F32)
    for i in range(NZ):
        pref[i] = total
        total = step_decay * total + got_ends[i]
    totals[x] = total
    for t in (xp, xm, x2):
        remote(totals.at[x], totals.at[x], st_send.at[1], st_recv.at[1], at(x_to=t)).start()
    w_step(2)
    settle(totals, NX - 1, st_recv.at[1])
    entering = jnp.zeros((1, CH), F32)
    for i in range(NX):
        gap = jnp.maximum(x - 1 - i, 0).astype(F32)
        used = jnp.where(i < x, 1.0, 0.0)
        entering = entering + used * jnp.exp(-own_rate * (float(ROWS * NZ) * gap)) * totals[i]
    for i in range(NZ):
        states[i] = pref[i] + jnp.exp(-own_rate * float(ROWS * i)) * entering
    got_states[z] = states[z]
    all_z(states, got_states, 2)
    w_step(3)
    w_step(4)
    settle(got_states, NZ - 1, st_recv.at[2])
    loads[3].wait()
    loads[5].wait()
    loads[6].wait()
    coef[...] = residue[...] * jnp.sqrt(2.0 * rate[...])

    a_pending = []
    partner = at(ch_to=y * NC + 1 - core)

    def a_copy(kind, g, block, where):
        part = a.at[block, g]
        return remote(part, part, a_send.at[kind, g], a_recv.at[kind, g], where)

    def a_go(kind, g, block, where):
        c = a_copy(kind, g, block, where)
        c.start()
        a_pending.append(c)

    up, down, far = at(ch_to=yp * NC + core), at(ch_to=ym * NC + core), y2 * NC + core
    from_up, from_down = yp * NC + core, ym * NC + core

    def a_make(g):
        lanes = slice(g * 128, (g + 1) * 128)
        ds = [rows_of(decay, m, lanes) for m in range(MODES)]
        cs = [rows_of(coef, m, lanes) for m in range(MODES)]
        hs = []
        for m in range(MODES):
            r = rows_of(rate, m, lanes) * float(LEN)
            into = jnp.broadcast_to(got_states[m, 0:1, lanes], (CHUNKS, 128))
            hs.append(carry[g, m] + jnp.exp(-r * chunk_f) * into)

        def scan2(o, hs):
            for u in range(2):
                where = pl.ds(o * 2 + u, CHUNKS, stride=LEN)
                s = sig[g, where, :]
                hs = [d * h + s for d, h in zip(ds, hs)]
                terms = [c * h for c, h in zip(cs, hs)]
                while len(terms) > 1:
                    terms = [p + r for p, r in zip(terms[::2], terms[1::2])]
                y_buf[where, :] = terms[0]
            return hs

        lax.fori_loop(0, LEN // 2, scan2, hs)
        conv = y_buf[...] + skip[0:1, lanes] * sig[g]
        a[ch, g] = (q[:, lanes].astype(F32) * conv).astype(BF16)
        a_go(1, g, ch, up)
        a_go(2, g, ch, down)
        a_go(0, g, ch, partner)

    def a_pass(g):
        a_copy(1, g, from_down, up).wait_recv()
        if g % 2 == 0:
            a_go(3, g, from_down, up)
        a_go(4, g, from_down, partner)
        a_copy(2, g, from_up, up).wait_recv()
        if g % 2 == 1:
            a_go(3, g, from_up, down)
        a_go(5, g, from_up, partner)

    def a_last(g):
        a_copy(3, g, far, up).wait_recv()
        a_go(6, g, far, partner)

    a_make(0)
    a_make(1)
    w_step(5)
    a_make(2)
    a_make(3)
    a_pass(0)
    w_step(6)
    a_pass(1)
    a_pass(2)
    a_last(0)
    w_step(7)
    a_pass(3)
    a_last(1)
    a_last(2)
    w_step(8)
    a_last(3)
    relay_step(8)

    for s in range(QR + 1):
        arrived(("x-", "r", s), q_part(back(s), xp))
        arrived(("x2", "r", s), q_part(back(s), x2))
    for s in range(1, QL + 1):
        arrived(("x+", "l", s), q_part(ahead(s), xm))
        arrived(("x2", "l", s), q_part(ahead(s), x2))
    other = 1 - core
    for kind, block in ((0, y), (4, ym), (5, yp), (6, y2)):
        for g in range(GROUPS):
            a_copy(kind, g, block * NC + other, partner).wait_recv()

    def multiply(j, _):
        left = jnp.concatenate([a[j, g] for g in range(GROUPS)], axis=1)
        first, x_at = (j % 2) * 8, j // 2
        for n in range(COLS // 256):
            cols = slice(n * 256, (n + 1) * 256)
            right = w[pl.ds(first, 8), x_at, :, cols].reshape(8 * WROWS, 256)
            acc[:, cols] += jnp.dot(left, right, preferred_element_type=F32)
        return 0

    acc[...] = jnp.zeros_like(acc)
    lax.fori_loop(0, NY * NC, multiply, 0)
    out[...] = acc[...].astype(BF16)

    settle(got_ends, NZ - 1, st_send.at[0])
    settle(totals, NX - 1, st_send.at[1])
    settle(got_states, NZ - 1, st_send.at[2])
    for c in pending + a_pending:
        c.wait_send()


def body(q_proj, k_proj, v_proj, residue, rate, skip, w_out):
    vmem = pl.BlockSpec(memory_space=pltpu.VMEM)
    hbm = pl.BlockSpec(memory_space=pl.ANY)
    dma = pltpu.SemaphoreType.DMA
    n_w = PR + PL + QR + QL + 3 * NZ + 3
    row = (1, CH)
    return pl.pallas_call(
        kernel,
        out_shape=jax.ShapeDtypeStruct((ROWS, COLS), BF16),
        in_specs=[hbm] * 7,
        out_specs=vmem,
        scratch_shapes=[
            pltpu.VMEM((ROWS, CH), BF16),
            pltpu.VMEM((ROWS, CH), BF16),
            pltpu.VMEM((ROWS, CH), BF16),
            pltpu.VMEM((MODES, CH), F32),
            pltpu.VMEM((MODES, CH), F32),
            pltpu.VMEM(row, F32),
            pltpu.VMEM((NZ, NX, WROWS, COLS), BF16),
            pltpu.VMEM((NY * NC, GROUPS, ROWS, 128), BF16),
            pltpu.VMEM((GROUPS, ROWS, 128), F32),
            pltpu.VMEM((ROWS, 128), F32),
            pltpu.VMEM((GROUPS, MODES, CHUNKS, 128), F32),
            pltpu.VMEM((ROWS, COLS), F32),
            pltpu.VMEM((MODES, CH), F32),
            pltpu.VMEM((MODES, CH), F32),
            pltpu.VMEM((MODES,) + row, F32),
            pltpu.VMEM((NZ,) + row, F32),
            pltpu.VMEM((NX,) + row, F32),
            pltpu.VMEM((NZ,) + row, F32),
            pltpu.VMEM((MODES,) + row, F32),
            pltpu.VMEM((NZ,) + row, F32),
            dma((7,)),
            dma((3,)),
            dma((3,)),
            dma((n_w,)),
            dma((n_w,)),
            dma((7, GROUPS)),
            dma((7, GROUPS)),
        ],
        compiler_params=pltpu.CompilerParams(
            collective_id=0, has_side_effects=True
        ),
    )(q_proj, k_proj, v_proj, w_out, residue, rate, skip.reshape(1, CH))


def solution(mesh):
    placed = (
        P("ctx", "ch"),
        P("ctx", "ch"),
        P("ctx", "ch"),
        P(None, "ch"),
        P(None, "ch"),
        P("ch"),
        P("ctx", "ch"),
    )
    return jax.shard_map(
        body, mesh=mesh, in_specs=placed, out_specs=P("ctx", "ch"), check_vma=False
    )
```

```python
import jax
import jax.numpy as jnp
from jax import lax
from jax.experimental import pallas as pl
from jax.experimental.pallas import tpu as pltpu
from jax.sharding import PartitionSpec as P

MESH = pl.DeviceIdType.MESH
NX, NZ, NY, NC = 4, 16, 4, 2
ROWS, CH, MODES = 256, 512, 16
WROWS, COLS, PCOLS = 64, 768, 256
GROUPS, CHUNKS, LEN = 4, 8, 32
PR, PL, QR, QL = 8, 7, 7, 8
QCOLS = COLS - PCOLS
F32, BF16 = jnp.float32, jnp.bfloat16
EARLY = "".split()
PLAN = " ".join(
    (
        "I0 p0 q1 r0",
        "p1 E0 q2 r1",
        "p2 T0 q3 r2",
        "p3 q4 r3 H0",
        "m0 p4 m1 q5",
        "r4 m2 p5 m3",
        "b0 q6 r5 b1",
        "p6 b2 l0 q7",
        "r6 b3 l1 p7",
        "l2 q8 r7 l3",
        "p8 r8",
    )
).split()
NEAR = (1, 3, 4, NZ - 4, NZ - 3, NZ - 1)


def kernel(
    q_hbm, k_hbm, v_hbm, w_hbm, residue_hbm, rate_hbm, skip_hbm, out,
    q, k, v, residue, rate, skip, w_p, w_q, a, sig, y_buf, carry, acc, decay, coef,
    ends, got_ends, totals, states, got_states, pref,
    load_sem, known, st_send, st_recv, w_send, w_recv, a_send, a_recv,
):
    ctx, ch = lax.axis_index("ctx"), lax.axis_index("ch")
    x, z = ctx // NZ, ctx % NZ
    y, core = ch // NC, ch % NC
    xp, xm, x2 = (x + 1) % NX, (x + 3) % NX, (x + 2) % NX
    zp, zm = (z + 1) % NZ, (z + NZ - 1) % NZ
    yp, ym, y2 = (y + 1) % NY, (y + 3) % NY, (y + 2) % NY

    def at(x_to=None, z_to=None, ch_to=None):
        x_to = x if x_to is None else x_to
        z_to = z if z_to is None else z_to
        return (x_to * NZ + z_to, ch if ch_to is None else ch_to)

    def remote(src, dst, send, recv, where):
        return pltpu.make_async_remote_copy(
            src_ref=src, dst_ref=dst, send_sem=send, recv_sem=recv,
            device_id=where, device_id_type=MESH,
        )

    loads = [
        pltpu.make_async_copy(k_hbm, k, load_sem.at[0]),
        pltpu.make_async_copy(v_hbm, v, load_sem.at[1]),
        pltpu.make_async_copy(w_hbm.at[:, pl.ds(0, PCOLS)], w_p.at[z, x], load_sem.at[2]),
        pltpu.make_async_copy(w_hbm.at[:, pl.ds(PCOLS, QCOLS)], w_q.at[z, x], load_sem.at[7]),
        pltpu.make_async_copy(q_hbm, q, load_sem.at[3]),
        pltpu.make_async_copy(rate_hbm, rate, load_sem.at[4]),
        pltpu.make_async_copy(residue_hbm, residue, load_sem.at[5]),
        pltpu.make_async_copy(skip_hbm, skip, load_sem.at[6]),
    ]
    for c in loads:
        c.start()

    barrier = pltpu.get_barrier_semaphore()
    greet = [at(z_to=(z + i) % NZ) for i in NEAR]
    greet += [at(x_to=t) for t in (xp, xm, x2)]
    greet += [at(ch_to=yp * NC + core), at(ch_to=ym * NC + core), at(ch_to=y * NC + 1 - core)]
    for d in greet:
        pl.semaphore_signal(barrier, inc=1, device_id=d, device_id_type=MESH)

    chunk = lax.broadcasted_iota(jnp.int32, (CHUNKS, 128), 0)
    chunk_f = chunk.astype(F32)

    def rows_of(ref, m, lanes):
        return jnp.broadcast_to(ref[m : m + 1, lanes], (CHUNKS, 128))

    def shifted(val, n):
        return jnp.where(chunk >= n, pltpu.roll(val, n, 0), 0.0)

    def first_pass(g):
        lanes = slice(g * 128, (g + 1) * 128)
        sig[g] = k[:, lanes].astype(F32) * v[:, lanes].astype(F32)
        ds = [rows_of(decay, m, lanes) for m in range(MODES)]

        def scan1(o, hs, g=g, ds=ds):
            for u in range(4):
                s = sig[g, pl.ds(o * 4 + u, CHUNKS, stride=LEN), :]
                hs = [d * h + s for d, h in zip(ds, hs)]
            return hs

        hs = lax.fori_loop(0, LEN // 4, scan1, [jnp.zeros((CHUNKS, 128), F32)] * MODES)
        for m in range(MODES):
            r = rows_of(rate, m, lanes) * float(LEN)
            end = jnp.sum(hs[m] * jnp.exp(-r * (CHUNKS - 1.0 - chunk_f)), axis=0, keepdims=True)
            ends[m, 0:1, lanes] = end
            c1 = jnp.exp(-r)
            val = shifted(hs[m], 1)
            val = val + c1 * shifted(val, 1)
            c2 = c1 * c1
            val = val + c2 * shifted(val, 2)
            val = val + (c2 * c2) * shifted(val, 4)
            carry[g, m] = val


    def all_z(src, dst, n):
        def one(i, _):
            to = (z + i) % NZ
            remote(src.at[to], dst.at[z], st_send.at[n], st_recv.at[n], at(z_to=to)).start()
            return 0

        lax.fori_loop(1, NZ, one, 0)

    def settle(ref, count, sem):
        part = ref.at[pl.ds(0, count)]
        pltpu.make_async_copy(part, part, sem).wait()

    keys = {}

    def slot(key):
        return keys.setdefault(key, len(keys))

    pending = []

    def w_copy(key, part, where):
        n = slot(key)
        return remote(part, part, w_send.at[n], w_recv.at[n], where)

    def send(key, part, where):
        c = w_copy(key, part, where)
        c.start()
        pending.append(c)

    def arrived(key, part):
        w_copy(key, part, at(z_to=zp)).wait_recv()

    def q_part(z_at, x_at):
        return w_q.at[z_at, x_at]

    def p_part(z_at, half):
        return w_p.at[z_at, pl.ds(2 * half, 2)]

    def back(s):
        return (z + NZ - s) % NZ

    def ahead(s):
        return (z + s) % NZ

    def across(way, s, z_at):
        part = q_part(z_at, x)
        send(("x+", way, s), part, at(x_to=xp))
        send(("x-", way, s), part, at(x_to=xm))

    def relay(way, s):
        if way == "r":
            z_at = back(s)
            part = q_part(z_at, xm)
            arrived(("x+", way, s), part)
            send(("x2", way, s), part, at(x_to=xp))
        else:
            z_at = ahead(s)
            part = q_part(z_at, xp)
            arrived(("x-", way, s), part)
            send(("x2", way, s), part, at(x_to=xm))

    def q_step(s):
        if s <= QR:
            if s:
                arrived(("qr", s - 1), q_part(back(s), x))
            if s < QR:
                send(("qr", s), q_part(back(s), x), at(z_to=zp))
        if s <= QL:
            if s:
                arrived(("ql", s - 1), q_part(ahead(s), x))
            if s < QL:
                send(("ql", s), q_part(ahead(s), x), at(z_to=zm))
        if s <= QR:
            across("r", s, back(s))
        if 0 < s <= QL:
            across("l", s, ahead(s))

    def p_step(s):
        for half in range(2):
            if s <= PR:
                if s:
                    arrived(("pr", s - 1, half), p_part(back(s), half))
                if s < PR:
                    send(("pr", s, half), p_part(back(s), half), at(z_to=zp))
            if s <= PL:
                if s:
                    arrived(("pl", s - 1, half), p_part(ahead(s), half))
                if s < PL:
                    send(("pl", s, half), p_part(ahead(s), half), at(z_to=zm))

    def relay_step(s):
        if s <= QR:
            relay("r", s)
        if 0 < s <= QL:
            relay("l", s)

    def p_ready():
        for key, x_from in (("p+", xm), ("p-", xp), ("p2", x2)):
            arrived((key,), w_p.at[z, x_from])

    def take_ends():
        settle(got_ends, NZ - 1, st_recv.at[0])
        own_rate = rate[pl.ds(z, 1), :]
        step_decay = jnp.exp(-own_rate * float(ROWS))
        total = jnp.zeros((1, CH), F32)
        for i in range(NZ):
            pref[i] = total
            total = step_decay * total + got_ends[i]
        totals[x] = total
        for t in (xp, xm, x2):
            remote(totals.at[x], totals.at[x], st_send.at[1], st_recv.at[1], at(x_to=t)).start()

    def take_totals():
        own_rate = rate[pl.ds(z, 1), :]
        settle(totals, NX - 1, st_recv.at[1])
        entering = jnp.zeros((1, CH), F32)
        for i in range(NX):
            gap = jnp.maximum(x - 1 - i, 0).astype(F32)
            used = jnp.where(i < x, 1.0, 0.0)
            entering = entering + used * jnp.exp(-own_rate * (float(ROWS * NZ) * gap)) * totals[i]
        for i in range(NZ):
            states[i] = pref[i] + jnp.exp(-own_rate * float(ROWS * i)) * entering
        got_states[z] = states[z]
        all_z(states, got_states, 2)

    def take_states():
        settle(got_states, NZ - 1, st_recv.at[2])
        loads[4].wait()
        loads[6].wait()
        loads[7].wait()
        coef[...] = residue[...] * jnp.sqrt(2.0 * rate[...])

    a_pending = []
    partner = at(ch_to=y * NC + 1 - core)

    def a_copy(kind, g, block, where):
        part = a.at[block, g]
        return remote(part, part, a_send.at[kind, g], a_recv.at[kind, g], where)

    def a_go(kind, g, block, where):
        c = a_copy(kind, g, block, where)
        c.start()
        a_pending.append(c)

    up, down, far = at(ch_to=yp * NC + core), at(ch_to=ym * NC + core), y2 * NC + core
    from_up, from_down = yp * NC + core, ym * NC + core

    def a_make(g):
        lanes = slice(g * 128, (g + 1) * 128)
        ds = [rows_of(decay, m, lanes) for m in range(MODES)]
        cs = [rows_of(coef, m, lanes) for m in range(MODES)]
        hs = []
        for m in range(MODES):
            r = rows_of(rate, m, lanes) * float(LEN)
            into = jnp.broadcast_to(got_states[m, 0:1, lanes], (CHUNKS, 128))
            hs.append(carry[g, m] + jnp.exp(-r * chunk_f) * into)

        def scan2(o, hs):
            for u in range(2):
                where = pl.ds(o * 2 + u, CHUNKS, stride=LEN)
                s = sig[g, where, :]
                hs = [d * h + s for d, h in zip(ds, hs)]
                terms = [c * h for c, h in zip(cs, hs)]
                while len(terms) > 1:
                    terms = [p + r for p, r in zip(terms[::2], terms[1::2])]
                y_buf[where, :] = terms[0]
            return hs

        lax.fori_loop(0, LEN // 2, scan2, hs)
        conv = y_buf[...] + skip[0:1, lanes] * sig[g]
        a[ch, g] = (q[:, lanes].astype(F32) * conv).astype(BF16)
        a_go(1, g, ch, up)
        a_go(2, g, ch, down)
        a_go(0, g, ch, partner)

    def a_pass(g):
        a_copy(1, g, from_down, up).wait_recv()
        if g % 2 == 0:
            a_go(3, g, from_down, up)
        a_go(4, g, from_down, partner)
        a_copy(2, g, from_up, up).wait_recv()
        if g % 2 == 1:
            a_go(3, g, from_up, down)
        a_go(5, g, from_up, partner)

    def a_last(g):
        a_copy(3, g, far, up).wait_recv()
        a_go(6, g, far, partner)

    near = z // 2

    def multiply(pair):
        half, g = pair // GROUPS, pair % GROUPS
        left = jnp.concatenate([a[i * NC + half, g] for i in range(NX)], axis=1)
        for n in range(COLS // 256):
            cols = slice(n * 256, (n + 1) * 256)
            src, first = (w_p, 0) if n == 0 else (w_q, (n - 1) * 256)
            right = jnp.concatenate(
                [
                    src[pl.ds(2 * pair, 2), i, :, first : first + 256].reshape(2 * WROWS, 256)
                    for i in range(NX)
                ],
                axis=0,
            )
            acc[:, cols] += jnp.dot(left, right, preferred_element_type=F32)

    def settled(s):
        if s <= QR:
            arrived(("x-", "r", s), q_part(back(s), xp))
            arrived(("x2", "r", s), q_part(back(s), x2))
        if 0 < s <= QL:
            arrived(("x+", "l", s), q_part(ahead(s), xm))
            arrived(("x2", "l", s), q_part(ahead(s), x2))

    def products(n):
        def one(i, _):
            multiply((near + i + 8 - n) % 8)
            return 0

        lax.fori_loop(0, 2 * n + 1, one, 0)

    steps = {
        "p": p_step, "q": q_step, "r": relay_step, "m": a_make, "b": a_pass, "l": a_last,
        "I": lambda n: p_ready(), "E": lambda n: take_ends(),
        "T": lambda n: take_totals(), "H": lambda n: take_states(),
        "w": lambda n: settled(n), "x": lambda n: products(n),
    }

    def run(plan):
        for op in plan:
            steps[op[0]](int(op[1:]))

    loads[2].wait()
    loads[3].wait()
    pl.semaphore_wait(barrier, len(greet))
    for n, i in enumerate(NEAR):
        pl.semaphore_signal(
            known.at[n], inc=1, device_id=at(z_to=(z + i) % NZ), device_id_type=MESH
        )
    for key, x_to in (("p+", xp), ("p-", xm), ("p2", x2)):
        send((key,), w_p.at[z, x], at(x_to=x_to))
    q_step(0)
    loads[5].wait()
    decay[...] = jnp.exp(-rate[...])
    loads[0].wait()
    loads[1].wait()
    first_pass(0)
    first_pass(1)
    run(EARLY)
    first_pass(2)
    first_pass(3)
    got_ends[z] = ends[z]
    for n in range(len(NEAR)):
        pl.semaphore_wait(known.at[n], 1)
    all_z(ends, got_ends, 0)
    run(PLAN)

    other = 1 - core
    for kind, block in ((0, y), (4, ym), (5, yp), (6, y2)):
        for g in range(GROUPS):
            a_copy(kind, g, block * NC + other, partner).wait_recv()

    acc[...] = jnp.zeros_like(acc)
    for s in range(6):
        settled(s)
    products(2)
    settled(6)
    settled(7)
    multiply((near + 3) % 8)
    multiply((near + 5) % 8)
    settled(8)
    multiply((near + 4) % 8)
    out[...] = acc[...].astype(BF16)

    settle(got_ends, NZ - 1, st_send.at[0])
    settle(totals, NX - 1, st_send.at[1])
    settle(got_states, NZ - 1, st_send.at[2])
    for c in pending + a_pending:
        c.wait_send()


def body(q_proj, k_proj, v_proj, residue, rate, skip, w_out):
    vmem = pl.BlockSpec(memory_space=pltpu.VMEM)
    hbm = pl.BlockSpec(memory_space=pltpu.HBM)
    dma = pltpu.SemaphoreType.DMA
    n_w = 2 * (PR + PL) + QR + QL + 3 * NZ + 3
    row = (1, CH)
    return pl.pallas_call(
        kernel,
        out_shape=jax.ShapeDtypeStruct((ROWS, COLS), BF16),
        in_specs=[hbm] * 7,
        out_specs=vmem,
        scratch_shapes=[
            pltpu.VMEM((ROWS, CH), BF16),
            pltpu.VMEM((ROWS, CH), BF16),
            pltpu.VMEM((ROWS, CH), BF16),
            pltpu.VMEM((MODES, CH), F32),
            pltpu.VMEM((MODES, CH), F32),
            pltpu.VMEM(row, F32),
            pltpu.VMEM((NZ, NX, WROWS, PCOLS), BF16),
            pltpu.VMEM((NZ, NX, WROWS, QCOLS), BF16),
            pltpu.VMEM((NY * NC, GROUPS, ROWS, 128), BF16),
            pltpu.VMEM((GROUPS, ROWS, 128), F32),
            pltpu.VMEM((ROWS, 128), F32),
            pltpu.VMEM((GROUPS, MODES, CHUNKS, 128), F32),
            pltpu.VMEM((ROWS, COLS), F32),
            pltpu.VMEM((MODES, CH), F32),
            pltpu.VMEM((MODES, CH), F32),
            pltpu.VMEM((MODES,) + row, F32),
            pltpu.VMEM((NZ,) + row, F32),
            pltpu.VMEM((NX,) + row, F32),
            pltpu.VMEM((NZ,) + row, F32),
            pltpu.VMEM((MODES,) + row, F32),
            pltpu.VMEM((NZ,) + row, F32),
            dma((8,)),
            pltpu.SemaphoreType.REGULAR((6,)),
            dma((3,)),
            dma((3,)),
            dma((n_w,)),
            dma((n_w,)),
            dma((7, GROUPS)),
            dma((7, GROUPS)),
        ],
        compiler_params=pltpu.CompilerParams(
            collective_id=0, has_side_effects=True, vmem_limit_bytes=48 * 2**20
        ),
    )(*[pltpu.with_memory_space_constraint(i, pltpu.HBM) for i in (q_proj, k_proj, v_proj, w_out, residue, rate, skip.reshape(1, CH))])


def solution(mesh):
    placed = (
        P("ctx", "ch"),
        P("ctx", "ch"),
        P("ctx", "ch"),
        P(None, "ch"),
        P(None, "ch"),
        P("ch"),
        P("ctx", "ch"),
    )
    return jax.shard_map(
        body, mesh=mesh, in_specs=placed, out_specs=P("ctx", "ch"), check_vma=False
    )
```

```python
import jax
import jax.numpy as jnp
from jax import lax
from jax.experimental import pallas as pl
from jax.experimental.pallas import tpu as pltpu
from jax.sharding import PartitionSpec as P

MESH = pl.DeviceIdType.MESH
NX, NZ, NY, NC = 4, 16, 4, 2
ROWS, CH, MODES = 256, 512, 16
WROWS, COLS, PCOLS = 64, 768, 256
GROUPS, CHUNKS, LEN = 4, 8, 32
PR, PL, QR, QL = 8, 7, 7, 8
QCOLS = COLS - PCOLS
F32, BF16 = jnp.float32, jnp.bfloat16
EARLY = "".split()
PLAN = " ".join(
    (
        "I0 p0 q1 p1",
        "r0 E0 q2 T0",
        "p2 r1 q3 p3",
        "r2 H0 q4 m0",
        "p4 m1 r3 m2",
        "q5 m3 p5 r4",
        "b0 q6 b1 p6",
        "r5 b2 l0 q7",
        "b3 l1 p7 r6",
        "l2 q8 l3 p8",
        "r7 r8",
    )
).split()
NEAR = (1, 3, 4, NZ - 4, NZ - 3, NZ - 1)


def kernel(
    q_hbm, k_hbm, v_hbm, w_hbm, residue_hbm, rate_hbm, skip_hbm, out,
    q, k, v, residue, rate, skip, w_p, w_q, a, sig, y_buf, carry, acc, decay, coef,
    ends, got_ends, totals, states, got_states, pref,
    load_sem, known, st_send, st_recv, w_send, w_recv, a_send, a_recv,
):
    ctx, ch = lax.axis_index("ctx"), lax.axis_index("ch")
    x, z = ctx // NZ, ctx % NZ
    y, core = ch // NC, ch % NC
    xp, xm, x2 = (x + 1) % NX, (x + 3) % NX, (x + 2) % NX
    zp, zm = (z + 1) % NZ, (z + NZ - 1) % NZ
    yp, ym, y2 = (y + 1) % NY, (y + 3) % NY, (y + 2) % NY

    def at(x_to=None, z_to=None, ch_to=None):
        x_to = x if x_to is None else x_to
        z_to = z if z_to is None else z_to
        return (x_to * NZ + z_to, ch if ch_to is None else ch_to)

    def remote(src, dst, send, recv, where):
        return pltpu.make_async_remote_copy(
            src_ref=src, dst_ref=dst, send_sem=send, recv_sem=recv,
            device_id=where, device_id_type=MESH,
        )

    loads = [
        pltpu.make_async_copy(k_hbm, k, load_sem.at[0]),
        pltpu.make_async_copy(v_hbm, v, load_sem.at[1]),
        pltpu.make_async_copy(w_hbm.at[:, pl.ds(0, PCOLS)], w_p.at[z, x], load_sem.at[2]),
        pltpu.make_async_copy(w_hbm.at[:, pl.ds(PCOLS, QCOLS)], w_q.at[z, x], load_sem.at[7]),
        pltpu.make_async_copy(q_hbm, q, load_sem.at[3]),
        pltpu.make_async_copy(rate_hbm, rate, load_sem.at[4]),
        pltpu.make_async_copy(residue_hbm, residue, load_sem.at[5]),
        pltpu.make_async_copy(skip_hbm, skip, load_sem.at[6]),
    ]
    for c in loads:
        c.start()

    barrier = pltpu.get_barrier_semaphore()
    greet = [at(z_to=(z + i) % NZ) for i in NEAR]
    greet += [at(x_to=t) for t in (xp, xm, x2)]
    greet += [at(ch_to=yp * NC + core), at(ch_to=ym * NC + core), at(ch_to=y * NC + 1 - core)]
    for d in greet:
        pl.semaphore_signal(barrier, inc=1, device_id=d, device_id_type=MESH)

    chunk = lax.broadcasted_iota(jnp.int32, (CHUNKS, 128), 0)
    chunk_f = chunk.astype(F32)

    def rows_of(ref, m, lanes):
        return jnp.broadcast_to(ref[m : m + 1, lanes], (CHUNKS, 128))

    def shifted(val, n):
        return jnp.where(chunk >= n, pltpu.roll(val, n, 0), 0.0)

    def first_pass(g):
        lanes = slice(g * 128, (g + 1) * 128)
        sig[g] = k[:, lanes].astype(F32) * v[:, lanes].astype(F32)
        ds = [rows_of(decay, m, lanes) for m in range(MODES)]

        def scan1(o, hs, g=g, ds=ds):
            for u in range(4):
                s = sig[g, pl.ds(o * 4 + u, CHUNKS, stride=LEN), :]
                hs = [d * h + s for d, h in zip(ds, hs)]
            return hs

        hs = lax.fori_loop(0, LEN // 4, scan1, [jnp.zeros((CHUNKS, 128), F32)] * MODES)
        for m in range(MODES):
            r = rows_of(rate, m, lanes) * float(LEN)
            end = jnp.sum(hs[m] * jnp.exp(-r * (CHUNKS - 1.0 - chunk_f)), axis=0, keepdims=True)
            ends[m, 0:1, lanes] = end
            c1 = jnp.exp(-r)
            val = shifted(hs[m], 1)
            val = val + c1 * shifted(val, 1)
            c2 = c1 * c1
            val = val + c2 * shifted(val, 2)
            val = val + (c2 * c2) * shifted(val, 4)
            carry[g, m] = val


    def all_z(src, dst, n):
        def one(i, _):
            to = (z + i) % NZ
            remote(src.at[to], dst.at[z], st_send.at[n], st_recv.at[n], at(z_to=to)).start()
            return 0

        lax.fori_loop(1, NZ, one, 0)

    def settle(ref, count, sem):
        part = ref.at[pl.ds(0, count)]
        pltpu.make_async_copy(part, part, sem).wait()

    keys = {}

    def slot(key):
        return keys.setdefault(key, len(keys))

    pending = []

    def w_copy(key, part, where):
        n = slot(key)
        return remote(part, part, w_send.at[n], w_recv.at[n], where)

    def send(key, part, where):
        c = w_copy(key, part, where)
        c.start()
        pending.append(c)

    def arrived(key, part):
        w_copy(key, part, at(z_to=zp)).wait_recv()

    def q_part(z_at, x_at):
        return w_q.at[z_at, x_at]

    def p_part(z_at, half):
        return w_p.at[z_at, pl.ds(2 * half, 2)]

    def back(s):
        return (z + NZ - s) % NZ

    def ahead(s):
        return (z + s) % NZ

    def across(way, s, z_at):
        part = q_part(z_at, x)
        send(("x+", way, s), part, at(x_to=xp))
        send(("x-", way, s), part, at(x_to=xm))

    def relay(way, s):
        if way == "r":
            z_at = back(s)
            part = q_part(z_at, xm)
            arrived(("x+", way, s), part)
            send(("x2", way, s), part, at(x_to=xp))
        else:
            z_at = ahead(s)
            part = q_part(z_at, xp)
            arrived(("x-", way, s), part)
            send(("x2", way, s), part, at(x_to=xm))

    def q_step(s):
        if s <= QR:
            if s:
                arrived(("qr", s - 1), q_part(back(s), x))
            if s < QR:
                send(("qr", s), q_part(back(s), x), at(z_to=zp))
        if s <= QL:
            if s:
                arrived(("ql", s - 1), q_part(ahead(s), x))
            if s < QL:
                send(("ql", s), q_part(ahead(s), x), at(z_to=zm))
        if s <= QR:
            across("r", s, back(s))
        if 0 < s <= QL:
            across("l", s, ahead(s))

    def p_step(s):
        for half in range(2):
            if s <= PR:
                if s:
                    arrived(("pr", s - 1, half), p_part(back(s), half))
                if s < PR:
                    send(("pr", s, half), p_part(back(s), half), at(z_to=zp))
            if s <= PL:
                if s:
                    arrived(("pl", s - 1, half), p_part(ahead(s), half))
                if s < PL:
                    send(("pl", s, half), p_part(ahead(s), half), at(z_to=zm))

    def relay_step(s):
        if s <= QR:
            relay("r", s)
        if 0 < s <= QL:
            relay("l", s)

    def p_ready():
        for key, x_from in (("p+", xm), ("p-", xp), ("p2", x2)):
            arrived((key,), w_p.at[z, x_from])

    def take_ends():
        settle(got_ends, NZ - 1, st_recv.at[0])
        own_rate = rate[pl.ds(z, 1), :]
        step_decay = jnp.exp(-own_rate * float(ROWS))
        total = jnp.zeros((1, CH), F32)
        for i in range(NZ):
            pref[i] = total
            total = step_decay * total + got_ends[i]
        totals[x] = total
        for t in (xp, xm, x2):
            remote(totals.at[x], totals.at[x], st_send.at[1], st_recv.at[1], at(x_to=t)).start()

    def take_totals():
        own_rate = rate[pl.ds(z, 1), :]
        settle(totals, NX - 1, st_recv.at[1])
        entering = jnp.zeros((1, CH), F32)
        for i in range(NX):
            gap = jnp.maximum(x - 1 - i, 0).astype(F32)
            used = jnp.where(i < x, 1.0, 0.0)
            entering = entering + used * jnp.exp(-own_rate * (float(ROWS * NZ) * gap)) * totals[i]
        for i in range(NZ):
            states[i] = pref[i] + jnp.exp(-own_rate * float(ROWS * i)) * entering
        got_states[z] = states[z]
        all_z(states, got_states, 2)

    def take_states():
        settle(got_states, NZ - 1, st_recv.at[2])
        loads[4].wait()
        loads[6].wait()
        loads[7].wait()
        coef[...] = residue[...] * jnp.sqrt(2.0 * rate[...])

    a_pending = []
    partner = at(ch_to=y * NC + 1 - core)

    def a_copy(kind, g, block, where):
        part = a.at[block, g]
        return remote(part, part, a_send.at[kind, g], a_recv.at[kind, g], where)

    def a_go(kind, g, block, where):
        c = a_copy(kind, g, block, where)
        c.start()
        a_pending.append(c)

    up, down, far = at(ch_to=yp * NC + core), at(ch_to=ym * NC + core), y2 * NC + core
    from_up, from_down = yp * NC + core, ym * NC + core

    def a_make(g):
        lanes = slice(g * 128, (g + 1) * 128)
        ds = [rows_of(decay, m, lanes) for m in range(MODES)]
        cs = [rows_of(coef, m, lanes) for m in range(MODES)]
        hs = []
        for m in range(MODES):
            r = rows_of(rate, m, lanes) * float(LEN)
            into = jnp.broadcast_to(got_states[m, 0:1, lanes], (CHUNKS, 128))
            hs.append(carry[g, m] + jnp.exp(-r * chunk_f) * into)

        def scan2(o, hs):
            for u in range(2):
                where = pl.ds(o * 2 + u, CHUNKS, stride=LEN)
                s = sig[g, where, :]
                hs = [d * h + s for d, h in zip(ds, hs)]
                terms = [c * h for c, h in zip(cs, hs)]
                while len(terms) > 1:
                    terms = [p + r for p, r in zip(terms[::2], terms[1::2])]
                y_buf[where, :] = terms[0]
            return hs

        lax.fori_loop(0, LEN // 2, scan2, hs)
        conv = y_buf[...] + skip[0:1, lanes] * sig[g]
        a[ch, g] = (q[:, lanes].astype(F32) * conv).astype(BF16)
        a_go(1, g, ch, up)
        a_go(2, g, ch, down)
        a_go(0, g, ch, partner)

    def a_pass(g):
        a_copy(1, g, from_down, up).wait_recv()
        if g % 2 == 0:
            a_go(3, g, from_down, up)
        a_go(4, g, from_down, partner)
        a_copy(2, g, from_up, up).wait_recv()
        if g % 2 == 1:
            a_go(3, g, from_up, down)
        a_go(5, g, from_up, partner)

    def a_last(g):
        a_copy(3, g, far, up).wait_recv()
        a_go(6, g, far, partner)

    near = z // 2

    def multiply(pair):
        half, g = pair // GROUPS, pair % GROUPS
        left = jnp.concatenate([a[i * NC + half, g] for i in range(NX)], axis=1)
        for n in range(COLS // 256):
            cols = slice(n * 256, (n + 1) * 256)
            src, first = (w_p, 0) if n == 0 else (w_q, (n - 1) * 256)
            right = jnp.concatenate(
                [
                    src[pl.ds(2 * pair, 2), i, :, first : first + 256].reshape(2 * WROWS, 256)
                    for i in range(NX)
                ],
                axis=0,
            )
            acc[:, cols] += jnp.dot(left, right, preferred_element_type=F32)

    def settled(s):
        if s <= QR:
            arrived(("x-", "r", s), q_part(back(s), xp))
            arrived(("x2", "r", s), q_part(back(s), x2))
        if 0 < s <= QL:
            arrived(("x+", "l", s), q_part(ahead(s), xm))
            arrived(("x2", "l", s), q_part(ahead(s), x2))

    def products(n):
        def one(i, _):
            multiply((near + i + 8 - n) % 8)
            return 0

        lax.fori_loop(0, 2 * n + 1, one, 0)

    steps = {
        "p": p_step, "q": q_step, "r": relay_step, "m": a_make, "b": a_pass, "l": a_last,
        "I": lambda n: p_ready(), "E": lambda n: take_ends(),
        "T": lambda n: take_totals(), "H": lambda n: take_states(),
        "w": lambda n: settled(n), "x": lambda n: products(n),
    }

    def run(plan):
        for op in plan:
            steps[op[0]](int(op[1:]))

    loads[2].wait()
    loads[3].wait()
    pl.semaphore_wait(barrier, len(greet))
    for n, i in enumerate(NEAR):
        pl.semaphore_signal(
            known.at[n], inc=1, device_id=at(z_to=(z + i) % NZ), device_id_type=MESH
        )
    for key, x_to in (("p+", xp), ("p-", xm), ("p2", x2)):
        send((key,), w_p.at[z, x], at(x_to=x_to))
    q_step(0)
    loads[5].wait()
    decay[...] = jnp.exp(-rate[...])
    loads[0].wait()
    loads[1].wait()
    first_pass(0)
    first_pass(1)
    run(EARLY)
    first_pass(2)
    first_pass(3)
    got_ends[z] = ends[z]
    for n in range(len(NEAR)):
        pl.semaphore_wait(known.at[n], 1)
    all_z(ends, got_ends, 0)
    run(PLAN)

    other = 1 - core
    for kind, block in ((0, y), (4, ym), (5, yp), (6, y2)):
        for g in range(GROUPS):
            a_copy(kind, g, block * NC + other, partner).wait_recv()

    acc[...] = jnp.zeros_like(acc)
    for s in range(6):
        settled(s)
    products(2)
    settled(6)
    settled(7)
    multiply((near + 3) % 8)
    multiply((near + 5) % 8)
    settled(8)
    multiply((near + 4) % 8)
    out[...] = acc[...].astype(BF16)

    settle(got_ends, NZ - 1, st_send.at[0])
    settle(totals, NX - 1, st_send.at[1])
    settle(got_states, NZ - 1, st_send.at[2])
    for c in pending + a_pending:
        c.wait_send()


def body(q_proj, k_proj, v_proj, residue, rate, skip, w_out):
    vmem = pl.BlockSpec(memory_space=pltpu.VMEM)
    hbm = pl.BlockSpec(memory_space=pltpu.HBM)
    dma = pltpu.SemaphoreType.DMA
    n_w = 2 * (PR + PL) + QR + QL + 3 * NZ + 3
    row = (1, CH)
    return pl.pallas_call(
        kernel,
        out_shape=jax.ShapeDtypeStruct((ROWS, COLS), BF16),
        in_specs=[hbm] * 7,
        out_specs=vmem,
        scratch_shapes=[
            pltpu.VMEM((ROWS, CH), BF16),
            pltpu.VMEM((ROWS, CH), BF16),
            pltpu.VMEM((ROWS, CH), BF16),
            pltpu.VMEM((MODES, CH), F32),
            pltpu.VMEM((MODES, CH), F32),
            pltpu.VMEM(row, F32),
            pltpu.VMEM((NZ, NX, WROWS, PCOLS), BF16),
            pltpu.VMEM((NZ, NX, WROWS, QCOLS), BF16),
            pltpu.VMEM((NY * NC, GROUPS, ROWS, 128), BF16),
            pltpu.VMEM((GROUPS, ROWS, 128), F32),
            pltpu.VMEM((ROWS, 128), F32),
            pltpu.VMEM((GROUPS, MODES, CHUNKS, 128), F32),
            pltpu.VMEM((ROWS, COLS), F32),
            pltpu.VMEM((MODES, CH), F32),
            pltpu.VMEM((MODES, CH), F32),
            pltpu.VMEM((MODES,) + row, F32),
            pltpu.VMEM((NZ,) + row, F32),
            pltpu.VMEM((NX,) + row, F32),
            pltpu.VMEM((NZ,) + row, F32),
            pltpu.VMEM((MODES,) + row, F32),
            pltpu.VMEM((NZ,) + row, F32),
            dma((8,)),
            pltpu.SemaphoreType.REGULAR((6,)),
            dma((3,)),
            dma((3,)),
            dma((n_w,)),
            dma((n_w,)),
            dma((7, GROUPS)),
            dma((7, GROUPS)),
        ],
        compiler_params=pltpu.CompilerParams(
            collective_id=0, has_side_effects=True, vmem_limit_bytes=48 * 2**20
        ),
    )(*[pltpu.with_memory_space_constraint(i, pltpu.HBM) for i in (q_proj, k_proj, v_proj, w_out, residue, rate, skip.reshape(1, CH))])


def solution(mesh):
    placed = (
        P("ctx", "ch"),
        P("ctx", "ch"),
        P("ctx", "ch"),
        P(None, "ch"),
        P(None, "ch"),
        P("ch"),
        P("ctx", "ch"),
    )
    return jax.shard_map(
        body, mesh=mesh, in_specs=placed, out_specs=P("ctx", "ch"), check_vma=False
    )
```
